32 devices in a mesh: groups: 2 (over x), rows: 16 (over z, y, core).
Axes of the slice: x: 2, y: 2, z: 4, core: 2. Of those that a mesh axis runs over, the one named last changes fastest.
Arguments:
- token_ids: int32 [1, 256], P(None, 'groups'), parts along dimension 1, may hold values from 0 to 32767
- parents: int32 [1, 8, 32], P(None, 'groups'), parts along dimension 1, may hold values from 0 to 31, as said below
- states: bfloat16 [256, 16, 128, 128], P(('groups', 'rows')), parts along dimension 0, may hold values from -1.75 to 1.75
- embed_table: bfloat16 [32768, 2048], P(None, 'rows'), may hold values from -6 to 6
- qkv_weight: bfloat16 [2048, 3, 2048], P(None, None, 'rows'), may hold values from -0.125 to 0.125
- gate_weight: float32 [16, 128], replicated, may hold values from -6 to 6
- gate_bias: float32 [16], replicated, may hold values from -2 to 3
- norm_gain: float32 [2048], replicated, may hold values from 0.1 to 1.9
- out_weight: bfloat16 [2048, 2048], P(None, 'rows'), may hold values from -0.125 to 0.125
Outputs:
- layer_out: bfloat16 [1, 256, 2048], P(None, 'groups', 'rows'), parts along dimension 1
- final_states: bfloat16 [256, 16, 128, 128], P(('groups', 'rows')), parts along dimension 0
The draws below stay inside these ranges and needn't reach their ends.
There are 2 independent parts, one for each index of `groups`. The reference program is written for one: setup_inputs(seed, part) draws one part's arguments, and reference() takes and returns one part's arrays. A program takes and returns all parts, laid end to end along the dimension named above; an argument that names none is the same for every part. Nothing has to cross between parts.
Inputs may be any that keep to these rules, and one draw needn't show every extreme that they name: The 32 beams of a user fall into 4 aligned blocks of 8. In every step and for every user, at most 2 children of one block have parents in any one other block, and in every step some user has exactly 2 children of one block with parents in another block.
All inputs are finite; a program needn't handle non-finite values.
Results may differ from the reference program's by a relative error of at most 0.0074.
Values may be sent and summed in bfloat16 or wider, within the bound.
A program may use at most 64 MiB of HBM per device.

```python
import math
import jax
import jax.numpy as jnp
import numpy as np
from jax import lax

HEADS = 16
HEAD = 128
VOCAB = 32768
BEAM = 32
CAP = 2
STEPS = 1
D = 2048
R_ALL = 128
USERS = 4


def draw_parents(key, part):
    key_list = jax.random.split(jax.random.fold_in(key, 11), 6)
    row_count = BEAM // 4
    shape_four = (STEPS, USERS, 4, row_count)
    counts = jax.random.randint(key_list[0], (STEPS, USERS, 4, 3), 0, CAP + 1)
    pick_dev = jax.random.randint(key_list[1], (STEPS, USERS, 1, 1), 0, 4)
    pick_off = jax.random.randint(key_list[2], (STEPS, USERS, 1, 1), 0, 3)
    dev_index = jnp.arange(4, dtype=jnp.int32)[None, None, :, None]
    off_index = jnp.arange(3, dtype=jnp.int32)[None, None, None, :]
    counts = jnp.where((dev_index == pick_dev) & (off_index == pick_off), CAP, counts)
    limits = jnp.cumsum(counts, axis=-1)
    slot_index = jnp.arange(row_count, dtype=jnp.int32)[None, None, None, :]
    offset = jnp.where(slot_index < limits[..., 0:1], 1, jnp.where(slot_index < limits[..., 1:2], 2, jnp.where(slot_index < limits[..., 2:3], 3, 0)))
    scores = jax.random.randint(key_list[3], shape_four, 0, 1 << 20) * row_count + slot_index
    ordering = jnp.argsort(scores, axis=-1, stable=True)
    offset = jnp.take_along_axis(offset, ordering, axis=-1)
    source = jnp.bitwise_xor(dev_index, offset)
    first_draw = jax.random.randint(key_list[4], shape_four, 0, row_count)
    second = jax.random.randint(key_list[5], shape_four, 0, row_count)
    within = jnp.minimum(first_draw, second)
    return (source * row_count + within).reshape(STEPS, USERS, BEAM).astype(jnp.int32)


def place_ends(array, rng, low, top_value):
    place = [jax.random.randint(jax.random.fold_in(rng, axis), (), 0, length) for axis, length in enumerate(array.shape)]
    main_axis = array.shape.index(max(array.shape))
    neighbour = place[:main_axis] + [(place[main_axis] + 1) % array.shape[main_axis]] + place[main_axis + 1:]
    return array.at[tuple(place)].set(low).at[tuple(neighbour)].set(top_value)


def block_levels(key, dims, shards, smallest, largest):
    level, own = 1.0, jax.random.fold_in(key, 6)
    for axis_at, parts in shards:
        steps = jnp.exp(jax.random.uniform(jax.random.fold_in(own, axis_at), (parts,), jnp.float32, smallest / len(shards), largest / len(shards)))
        level = level * jnp.repeat(steps, dims[axis_at] // parts).reshape([-1 if axis == axis_at else 1 for axis in range(len(dims))])
    return level


def cumulative_ranks(number_of, skew):
    loads = [(1 << 20) // math.isqrt(rank ** skew) + 1 for rank in range(1, number_of + 1)]
    scale = 1 + sum(loads) // (1 << 30)
    return np.cumsum(np.array([max(1, weight // scale) for weight in loads]))


def ranked(own_key, extent, amount, lean):
    grid = cumulative_ranks(amount, lean)
    lot = jax.random.randint(jax.random.fold_in(own_key, 1), extent, 0, int(grid[amount - 1]))
    rank = jnp.searchsorted(jnp.asarray(grid, jnp.int32), lot, side="right")
    return jax.random.permutation(jax.random.fold_in(own_key, 2), amount)[rank].astype(jnp.int32)


def scatter_about(stream_key, dims, spread, reach, shards=(), held_as=jnp.bfloat16):
    array = spread * jax.random.normal(stream_key, dims, jnp.float32)
    if shards:
        array = array * block_levels(stream_key, dims, shards, -0.22, 0.18)
    return jnp.clip(array, -reach, reach).astype(held_as)


def setup_inputs(seed: int = 0, part: int = 0) -> dict:
    seeds = jax.random.split(jax.random.key(seed), 10)
    part_splits = jax.random.split(jax.random.fold_in(seeds[9], part), 10)
    token_ids = place_ends(ranked(part_splits[0], (STEPS, R_ALL), VOCAB, 2), jax.random.fold_in(part_splits[0], 3), 0, VOCAB - 1).astype(jnp.int32)
    parents = draw_parents(jax.random.fold_in(jax.random.fold_in(seeds[9], part), 71), part)
    states = scatter_about(part_splits[2], (R_ALL, HEADS, HEAD, HEAD), 0.3, 1.75, ((0, 16),))
    embed_table = scatter_about(seeds[3], (VOCAB, D), 1.0, 6.0, ((1, 16),))
    qkv_weight = scatter_about(seeds[4], (D, 3, D), D ** -0.5, 0.125, ((2, 16),))
    gate_weight = scatter_about(seeds[5], (HEADS, HEAD), 1.0, 6.0, (), jnp.float32)
    gate_bias = jnp.clip(jax.random.uniform(seeds[6], (HEADS,), jnp.float32, -2.0, 3.0), -2.0, 3.0)
    norm_gain = jnp.clip(1.0 + 0.18 * jax.random.normal(seeds[7], (D,), jnp.float32), 0.1, 1.9)
    out_weight = scatter_about(seeds[8], (D, D), D ** -0.5, 0.125, ((1, 16),))
    return {"token_ids": token_ids, "parents": parents, "states": states, "embed_table": embed_table, "qkv_weight": qkv_weight, "gate_weight": gate_weight, "gate_bias": gate_bias, "norm_gain": norm_gain, "out_weight": out_weight}


def reference(token_ids, parents, states, embed_table, qkv_weight, gate_weight, gate_bias, norm_gain, out_weight):
    width = HEADS * HEAD
    row_count = USERS * BEAM
    weight_flat = qkv_weight.reshape(width, 3 * width)
    state_now = states
    outputs = []
    for step_index in range(STEPS):
        inputs = jnp.take(embed_table, token_ids[step_index], axis=0)
        projected = jnp.dot(inputs, weight_flat, preferred_element_type=jnp.float32).astype(jnp.bfloat16)
        projected = projected.reshape(row_count, 3, HEADS, HEAD)
        parent_rows = (jnp.arange(USERS, dtype=jnp.int32)[:, None] * BEAM + parents[step_index]).reshape(row_count)
        prior_state = jnp.take(state_now, parent_rows, axis=0)

        def update(block):
            prior_block, proj_block = block
            queries = proj_block[:, 0].astype(jnp.float32)
            key_float = proj_block[:, 1].astype(jnp.float32)
            values = proj_block[:, 2].astype(jnp.float32)
            gate_logit = lax.optimization_barrier(jnp.sum(key_float * gate_weight, axis=-1)) / math.sqrt(HEAD) + gate_bias
            decay_rate = jax.nn.sigmoid(gate_logit)
            key_unit = key_float * lax.rsqrt(lax.optimization_barrier(jnp.sum(key_float * key_float, axis=-1, keepdims=True)) + 1e-06)
            new_state = decay_rate[:, :, None, None] * prior_block.astype(jnp.float32) + key_unit[:, :, :, None] * values[:, :, None, :]
            new_state = new_state.astype(jnp.bfloat16)
            readout = jnp.einsum('bhd,bhde->bhe', queries, new_state.astype(jnp.float32))
            scaled = readout * lax.rsqrt(lax.optimization_barrier(jnp.mean(readout * readout, axis=-1, keepdims=True)) + 1e-05)
            normed = (scaled.reshape(BEAM, width) * norm_gain).astype(jnp.bfloat16)
            return (new_state, normed)
        new_states, normed = lax.map(update, (prior_state.reshape(USERS, BEAM, HEADS, HEAD, HEAD), projected.reshape(USERS, BEAM, 3, HEADS, HEAD)))
        state_now = new_states.reshape(row_count, HEADS, HEAD, HEAD)
        attention = jnp.dot(normed.reshape(row_count, width), out_weight, preferred_element_type=jnp.float32)
        outputs.append((inputs.astype(jnp.float32) + attention).astype(jnp.bfloat16))
    return (jnp.stack(outputs), state_now)
```

```python
import functools
import math

import jax
import jax.numpy as jnp
from jax import lax
from jax.experimental import pallas as pl
from jax.experimental.pallas import tpu as pltpu
from jax.sharding import PartitionSpec as P

CAP = 2
SPANS = (1, 3, 4, 8)
ANY = pl.BlockSpec(memory_space=pl.ANY)
VM = pl.BlockSpec(memory_space=pltpu.VMEM)
SM = pl.BlockSpec(memory_space=pltpu.SMEM)


def neighbours(count):
    me = lax.axis_index("rows")
    member, my_level = me % 4, me // 4
    side_member = (member + 2) % 4
    twin_member = member + 1 - 2 * (member % 2)
    diag_member = (twin_member + 2) % 4
    levels = [(my_level + k) % (count // 4) for k in range(1, count // 4)]
    return me, my_level, member, side_member, twin_member, diag_member, levels


def remote(source, target_ref, out_sem, in_sem, target):
    return pltpu.make_async_remote_copy(
        src_ref=source,
        dst_ref=target_ref,
        send_sem=out_sem,
        recv_sem=in_sem,
        device_id={"rows": target},
        device_id_type=pl.DeviceIdType.MESH,
    )


def across(row):
    size = row.shape[1]
    wide = jnp.broadcast_to(row, (size, size))
    here = lax.broadcasted_iota(jnp.int32, (size, size), 0)
    there = lax.broadcasted_iota(jnp.int32, (size, size), 1)
    return jnp.sum(jnp.where(here == there, wide, 0.0), axis=1, keepdims=True)


def layer_kernel(
    count, row_local, cuts, list_s, tok_s, bias_s, list_v, gate_v, gain_v, states, table, weights,
    out_weights, got, got_one, unit_o, value_o, decay_o, layer_o,
    st, sb, tab, wts, owts, wide, rows_f, every, proj, qkv, units, vals, decs, spread, slots,
    normed, unit_v, value_v, decay_v, layer_v, layer_b,
    load_sem, tab_sem, w_sem, o_sem, send_sem, bulk_send, bulk_recv, recv_a, recv_b, recv_c,
    recv_d
):
    me, my_level, member, side_m, twin_m, diag_m, levels = neighbours(count)
    side, twin, diag = (my_level * 4 + m for m in (side_m, twin_m, diag_m))
    heads, head_size = st.shape[1], st.shape[2]
    beams = 4 * row_local
    half = member % 2

    barrier = pltpu.get_barrier_semaphore()
    peers = [side, twin, diag] + [other * 4 + member for other in levels]
    for peer in peers:
        pl.semaphore_signal(
            barrier, inc=1, device_id={"rows": peer}, device_id_type=pl.DeviceIdType.MESH
        )
    state_loads = [
        pltpu.make_async_copy(states.at[row], st.at[row], load_sem.at[row])
        for row in range(row_local)
    ]
    for load in state_loads:
        load.start()
    pieces = tab_sem.shape[0]
    span = tab.shape[0] // pieces
    table_loads = [
        pltpu.make_async_copy(
            table.at[pl.ds(k * span, span)], tab.at[pl.ds(k * span, span)], tab_sem.at[k]
        )
        for k in range(pieces)
    ]
    for load in table_loads:
        load.start()
    weight_load = pltpu.make_async_copy(weights, wts, w_sem.at[0])
    weight_load.start()
    out_load = pltpu.make_async_copy(out_weights, owts, w_sem.at[1])
    out_load.start()

    chosen = []
    for partner in (2, 3, 1):
        target = (side_m, diag_m, twin_m)[(2, 3, 1).index(partner)]
        seen = jnp.int32(0)
        picks = [jnp.int32(0)] * CAP
        for child in range(row_local):
            parent = list_s[0, my_level, target * row_local + child]
            needed = lax.div(parent, row_local) == member
            for order in range(CAP):
                picks[order] = jnp.where(
                    needed & (seen == order), lax.rem(parent, row_local), picks[order]
                )
            seen = seen + needed.astype(jnp.int32)
        chosen += picks
    for load in state_loads:
        load.wait()
    for slot in range(3 * CAP):
        sb[slot] = st[chosen[slot]]
    pl.semaphore_wait(barrier, len(peers))

    sent, arriving = [], []

    def bulk(index):
        first, length = cuts[index]
        for slot in range(2 * CAP):
            at = index * 2 * CAP + slot
            copy = remote(
                sb.at[slot, pl.ds(first, length)], got.at[slot, pl.ds(first, length)],
                bulk_send.at[at], bulk_recv.at[at], side if slot < CAP else diag,
            )
            copy.start()
            arriving.append(copy)

    def send(source, target_ref, sem, target):
        copy = remote(source, target_ref, send_sem.at[len(sent)], sem, target)
        copy.start()
        sent.append(copy)

    def arrived(ref, sem):
        remote(ref, ref, send_sem.at[0], sem, twin).wait_recv()

    bulk(0)
    for load in table_loads:
        load.wait()
    tokens = rows_f.shape[0]

    def fetch(i, carry):
        wide[pl.ds(pl.multiple_of(i * 8, 8), 8), :] = tab[lax.div(tok_s[0, i], 8)].astype(
            jnp.float32
        )
        return carry

    def pick(i, carry):
        rows_f[pl.ds(i, 1), :] = wide[pl.ds(i * 8 + lax.rem(tok_s[0, i], 8), 1), :]
        return carry

    lax.fori_loop(0, tokens, fetch, 0, unroll=8)
    lax.fori_loop(0, tokens, pick, 0, unroll=8)
    every[me] = rows_f[...].astype(jnp.bfloat16)

    mine = every.at[me]
    send(mine, mine, recv_a.at[me], side)
    for other in levels:
        send(mine, mine, recv_a.at[me], other * 4 + member)
    send(mine, mine, recv_a.at[me], twin)
    bulk(1)

    def took(buffer, sems, block):
        arrived(buffer.at[block], sems.at[block])

    def forward(buffer, sems, block, target):
        send(buffer.at[block], buffer.at[block], sems.at[block], target)

    took(every, recv_a, side)
    for other in levels:
        forward(every, recv_a, side, other * 4 + member)
    forward(every, recv_a, side, twin)
    for column in (member, side_m):
        for other in levels:
            took(every, recv_a, other * 4 + column)
            forward(every, recv_a, other * 4 + column, twin)
    took(every, recv_a, twin)
    took(every, recv_a, diag)
    for column in (twin_m, diag_m):
        for other in levels:
            took(every, recv_a, other * 4 + column)

    weight_load.wait()
    lhs = jnp.concatenate([every[k] for k in range(count)], axis=1)
    for slab in range(3):
        done = jnp.dot(lhs, wts[slab], preferred_element_type=jnp.float32)
        done = done.astype(jnp.bfloat16)
        for level in range(count // 4):
            proj[level, :, slab * head_size : (slab + 1) * head_size] = done[
                level * beams : (level + 1) * beams
            ]

    own = proj.at[my_level]
    for other in levels:
        send(proj.at[other], qkv.at[me], recv_b.at[me], other * 4 + member)
    send(own, qkv.at[me], recv_b.at[me], side)
    send(own, qkv.at[me], recv_b.at[me], twin)
    qkv[me] = proj[my_level]
    for other in levels:
        took(qkv, recv_b, other * 4 + member)
        forward(qkv, recv_b, other * 4 + member, side)
        forward(qkv, recv_b, other * 4 + member, twin)
    bulk(2)
    for level in [my_level] + levels:
        took(qkv, recv_b, level * 4 + side_m)
        forward(qkv, recv_b, level * 4 + side_m, twin)

    lists = list_v[0, pl.ds(my_level, 1), :].astype(jnp.float32)
    place_row = lax.broadcasted_iota(jnp.int32, (1, beams), 1)
    place_col = lax.broadcasted_iota(jnp.int32, (beams, 1), 0)
    lists_row = lists.astype(jnp.int32)
    lists_col = across(lists).astype(jnp.int32)
    block_row, block_col = lax.div(place_row, row_local), lax.div(place_col, row_local)
    from_row, from_col = lax.div(lists_row, row_local), lax.div(lists_col, row_local)
    same = (block_row == block_col) & (from_row == from_col)
    rank_col = jnp.sum(
        jnp.where(same & (place_row < place_col), 1.0, 0.0), axis=1, keepdims=True
    ).astype(jnp.int32)
    rank_row = jnp.sum(
        jnp.where(same & (place_col < place_row), 1.0, 0.0), axis=0, keepdims=True
    ).astype(jnp.int32)
    off_row = jnp.bitwise_xor(block_row, from_row)
    off_col = jnp.bitwise_xor(block_col, from_col)
    slot_row = jnp.where(
        off_row == 0, lax.rem(place_row, row_local), row_local + (off_row - 1) * CAP + rank_row
    )
    slot_col = jnp.where(
        off_col == 0, lax.rem(place_col, row_local), row_local + (off_col - 1) * CAP + rank_col
    )
    slot_count = slots.shape[1]
    slot_index = lax.broadcasted_iota(jnp.int32, (slot_count, beams), 0)
    slot_pick = jnp.where(
        (from_row == member) & (slot_row == slot_index), 1.0, 0.0
    ).astype(jnp.bfloat16)
    wanted = from_col * slot_count + slot_col
    all_slots = lax.broadcasted_iota(jnp.int32, (beams, 4 * slot_count), 1)
    row_pick = jnp.where(wanted == all_slots, 1.0, 0.0)
    row_pick = jnp.concatenate(
        [
            row_pick[m * row_local : (m + 1) * row_local]
            for m in (0, 2, 1, 3)
        ],
        axis=0,
    ).astype(jnp.bfloat16)
    held = jnp.broadcast_to(from_col == member, (beams, head_size))
    within = jnp.broadcast_to(lax.rem(lists_col, row_local), (beams, head_size))
    masks = [held & (within == p) for p in range(row_local)]

    for column in (twin_m, diag_m):
        for level in [my_level] + levels:
            took(qkv, recv_b, level * 4 + column)
    for slot in range(CAP):
        copy = remote(
            sb.at[2 * CAP + slot], got_one.at[slot],
            bulk_send.at[len(cuts) * 2 * CAP + slot], bulk_recv.at[len(cuts) * 2 * CAP + slot],
            twin,
        )
        copy.start()
        arriving.append(copy)

    for head in range(heads):
        block = qkv[head]
        queries = block[:, :head_size].astype(jnp.float32)
        keys = block[:, head_size : 2 * head_size].astype(jnp.float32)
        values = block[:, 2 * head_size :].astype(jnp.float32)
        logit = jnp.sum(keys * gate_v[head : head + 1], axis=-1, keepdims=True)
        decay = jax.nn.sigmoid(logit / math.sqrt(head_size) + bias_s[head])
        unit = keys * lax.rsqrt(jnp.sum(keys * keys, axis=-1, keepdims=True) + 1e-06)
        spreadq = jnp.concatenate(
            [jnp.where(mask, queries, 0.0).astype(jnp.bfloat16) for mask in masks], axis=1
        )
        stacked = st[:, head].reshape(row_local * head_size, head_size)
        total = jnp.dot(spreadq, stacked, preferred_element_type=jnp.float32)
        readout = decay * total + jnp.sum(queries * unit, axis=-1, keepdims=True) * values
        scaled = readout * lax.rsqrt(jnp.mean(readout * readout, axis=-1, keepdims=True) + 1e-05)
        spread[:, head * head_size : (head + 1) * head_size] = (
            scaled * gain_v[head : head + 1]
        ).astype(jnp.bfloat16)
        units[head] = unit
        vals[head] = values
        decs[head] = jnp.broadcast_to(decay, (beams, head_size))
    slots[member] = jnp.dot(
        slot_pick, spread[...], preferred_element_type=jnp.float32
    ).astype(jnp.bfloat16)

    forward(slots, recv_c, member, side)
    forward(slots, recv_c, member, twin)
    bulk(3)
    for head in range(heads):
        here = pl.ds(pl.multiple_of(member * row_local, row_local), row_local)
        for target, source in ((unit_v, units), (value_v, vals), (decay_v, decs)):
            target[:, head : head + 1, :] = source[head, here, :].reshape(
                row_local, 1, head_size
            )
    took(slots, recv_c, side_m)
    forward(slots, recv_c, side_m, twin)
    took(slots, recv_c, twin_m)
    took(slots, recv_c, diag_m)
    level_rows = jnp.dot(
        row_pick, slots[...].reshape(4 * slot_count, heads * head_size),
        preferred_element_type=jnp.float32,
    ).astype(jnp.bfloat16)
    for core in range(2):
        normed[my_level * 2 + core] = level_rows[core * 2 * row_local : (core + 1) * 2 * row_local]
    for other in levels:
        forward(normed, recv_d, my_level * 2 + half, other * 4 + member)
    for other in levels:
        took(normed, recv_d, other * 2 + half)
        forward(normed, recv_d, other * 2 + half, twin)
    for other in levels:
        took(normed, recv_d, other * 2 + 1 - half)
    out_load.wait()
    attention = jnp.dot(
        normed[...].reshape(count * row_local, heads * head_size), owts[...],
        preferred_element_type=jnp.float32,
    )
    for level in range(count // 4):
        for core in range(2):
            for line in range(2):
                source = ((level * 2 + core) * 2 + line) * row_local
                target = ((level * 2 + line) * 2 + core) * row_local
                rows = slice(target, target + row_local)
                layer_v[rows] = rows_f[rows] + attention[source : source + row_local]
    layer_b[...] = layer_v[...].astype(jnp.bfloat16)
    outs = [
        pltpu.make_async_copy(source, target, o_sem.at[k])
        for k, (source, target) in enumerate(
            (
                (unit_v, unit_o), (value_v, value_o), (decay_v, decay_o), (layer_b, layer_o)
            )
        )
    ]
    for copy in sent:
        copy.wait_send()
    for copy in outs:
        copy.start()
    for copy in arriving:
        copy.wait()
    for copy in outs:
        copy.wait()


def layer(
    parents, tokens, gate_bias, gate_weight, norm_gain, states, table, weights, out_weight, count
):
    row_local, heads, head_size, _ = states.shape
    row_total, depth = tokens.shape[1], weights.shape[1]
    beams = parents.shape[2]
    slot_count = 16 * ((row_local + 3 * CAP + 15) // 16)
    cuts, first = [], 0
    for span in SPANS:
        cuts.append((first, span * heads // 16))
        first += span * heads // 16
    bulk = (len(cuts) * 2 + 1) * CAP
    sends = 64
    bf, f32 = jnp.bfloat16, jnp.float32
    dma = pltpu.SemaphoreType.DMA
    rows = (row_local, heads, head_size)
    return pl.pallas_call(
        functools.partial(layer_kernel, count, row_local, tuple(cuts)),
        out_shape=(
            jax.ShapeDtypeStruct((2 * CAP,) + states.shape[1:], states.dtype),
            jax.ShapeDtypeStruct((CAP,) + states.shape[1:], states.dtype),
            jax.ShapeDtypeStruct(rows, f32),
            jax.ShapeDtypeStruct(rows, f32),
            jax.ShapeDtypeStruct(rows, f32),
            jax.ShapeDtypeStruct((row_total, head_size), bf),
        ),
        in_specs=[SM, SM, SM, VM, VM, VM, ANY, ANY, ANY, ANY],
        out_specs=(ANY,) * 6,
        scratch_shapes=[
            pltpu.VMEM(states.shape, bf),
            pltpu.VMEM((3 * CAP,) + states.shape[1:], bf),
            pltpu.VMEM((table.shape[0] // 8, 8, head_size), bf),
            pltpu.VMEM(weights.shape, bf),
            pltpu.VMEM(out_weight.shape, bf),
            pltpu.VMEM((row_total * 8, head_size), f32),
            pltpu.VMEM((row_total, head_size), f32),
            pltpu.VMEM((count, row_total, head_size), bf),
            pltpu.VMEM((count // 4, beams, 3 * head_size), bf),
            pltpu.VMEM((count, beams, 3 * head_size), bf),
            pltpu.VMEM((heads, beams, head_size), f32),
            pltpu.VMEM((heads, beams, head_size), f32),
            pltpu.VMEM((heads, beams, head_size), f32),
            pltpu.VMEM((beams, heads * head_size), bf),
            pltpu.VMEM((4, slot_count, heads * head_size), bf),
            pltpu.VMEM((count // 2, 2 * row_local, heads * head_size), bf),
            pltpu.VMEM(rows, f32),
            pltpu.VMEM(rows, f32),
            pltpu.VMEM(rows, f32),
            pltpu.VMEM((row_total, head_size), f32),
            pltpu.VMEM((row_total, head_size), bf),
            dma((row_local,)),
            dma((4,)),
            dma((2,)),
            dma((4,)),
            dma((sends,)),
            dma((bulk,)),
            dma((bulk,)),
            dma((count,)),
            dma((count,)),
            dma((4,)),
            dma((count // 2,)),
        ],
        compiler_params=pltpu.CompilerParams(collective_id=1, has_side_effects=True),
        name="layer_step",
    )(
        parents, tokens, gate_bias, parents, gate_weight, norm_gain.reshape(heads, head_size),
        states, table.reshape(table.shape[0] // 8, 8, head_size), weights, out_weight,
    )


def update_kernel(
    list_s, states, got, got_one, units, values, decays, layer_in, out_ref, layer_out,
    old, new, unit_v, value_v, decay_v, layer_v, in_sem, out_sem, side_sem
):
    row_local, heads = old.shape[0], old.shape[1]
    device = lax.axis_index("rows")
    member, user = device % 4, device // 4
    sides = [
        pltpu.make_async_copy(source, target, side_sem.at[k])
        for k, (source, target) in enumerate(
            ((units, unit_v), (values, value_v), (decays, decay_v), (layer_in, layer_v))
        )
    ]
    for copy in sides:
        copy.start()
    parents = [list_s[0, user, member * row_local + row] for row in range(row_local)]
    blocks = [lax.div(parent, row_local) for parent in parents]
    for row in range(row_local):
        partner = jnp.bitwise_xor(blocks[row], member)
        rank = jnp.int32(0)
        for earlier in range(row):
            rank = rank + (blocks[earlier] == blocks[row]).astype(jnp.int32)

        @pl.when(partner == 0)
        def _():
            pltpu.make_async_copy(
                states.at[lax.rem(parents[row], row_local)], old.at[row], in_sem.at[row]
            ).start()

        @pl.when(partner == 1)
        def _():
            pltpu.make_async_copy(got_one.at[rank], old.at[row], in_sem.at[row]).start()

        @pl.when(partner > 1)
        def _():
            pltpu.make_async_copy(
                got.at[(partner - 2) * CAP + rank], old.at[row], in_sem.at[row]
            ).start()

    for copy in sides:
        copy.wait()
    last = pltpu.make_async_copy(layer_v, layer_out, side_sem.at[0])
    last.start()

    def step(row, carry):
        pltpu.make_async_copy(states.at[0], old.at[row], in_sem.at[row]).wait()
        columns = jnp.transpose(unit_v[row])
        value = value_v[row]
        decay = decay_v[row]
        for head in range(heads):
            fresh = columns[:, head : head + 1] * value[head : head + 1, :]
            prior = old[row, head].astype(jnp.float32)
            new[row, head] = (decay[head : head + 1, :] * prior + fresh).astype(jnp.bfloat16)
        pltpu.make_async_copy(new.at[row], out_ref.at[row], out_sem.at[row]).start()
        return carry

    lax.fori_loop(0, row_local, step, 0)
    for row in range(row_local):
        pltpu.make_async_copy(new.at[row], out_ref.at[row], out_sem.at[row]).wait()
    last.wait()


def update(parents, states, got, got_one, units, values, decays, layer_in):
    row_local = states.shape[0]
    return pl.pallas_call(
        update_kernel,
        out_shape=(
            jax.ShapeDtypeStruct(states.shape, states.dtype),
            jax.ShapeDtypeStruct(layer_in.shape, layer_in.dtype),
        ),
        in_specs=[SM] + [ANY] * 7,
        out_specs=(ANY, ANY),
        scratch_shapes=[
            pltpu.VMEM(states.shape, states.dtype),
            pltpu.VMEM(states.shape, states.dtype),
            pltpu.VMEM(units.shape, units.dtype),
            pltpu.VMEM(values.shape, values.dtype),
            pltpu.VMEM(decays.shape, decays.dtype),
            pltpu.VMEM(layer_in.shape, layer_in.dtype),
            pltpu.SemaphoreType.DMA((row_local,)),
            pltpu.SemaphoreType.DMA((row_local,)),
            pltpu.SemaphoreType.DMA((4,)),
        ],
        cost_estimate=pl.CostEstimate(
            flops=4 * math.prod(states.shape),
            bytes_accessed=4 * math.prod(states.shape),
            transcendentals=0,
        ),
        name="update_states",
    )(parents, states, got, got_one, units, values, decays, layer_in)


def fast(
    token_ids, parents, states, embed_table, qkv_weight, gate_weight, gate_bias, norm_gain,
    out_weight
):
    count = lax.axis_size("rows")
    got, got_one, units, values, decays, layer_mid = layer(
        parents, token_ids, gate_bias, gate_weight, norm_gain, states, embed_table,
        jnp.transpose(qkv_weight, (1, 0, 2)), out_weight, count,
    )
    state_now, layer_out = update(
        parents, states, got, got_one, units, values, decays, layer_mid
    )
    return (layer_out[None], state_now)


def from_partner(block, axis, stride):
    count = lax.axis_size(axis)
    route = []
    for low in range(count):
        high = low | 1 << stride
        if high != low and high < count:
            route += [(low, high), (high, low)]
    return lax.ppermute(block, axis, route)


def outgoing(state_now, parent_list, member, row_local, partner):
    target = jnp.bitwise_xor(member, partner)
    children = lax.dynamic_slice_in_dim(parent_list, target * row_local, row_local, 0)
    needed = children // row_local == member
    rank_index = jnp.cumsum(needed.astype(jnp.int32)) - 1
    slot_ids = jnp.arange(CAP, dtype=jnp.int32)
    chosen = jnp.sum(
        jnp.where(
            needed[None, :] & (rank_index[None, :] == slot_ids[:, None]),
            (children % row_local)[None, :],
            0,
        ),
        axis=1,
    )
    return jnp.take(state_now, chosen, axis=0)


def route(state_now, parent_list, member, row_local):
    first_out = outgoing(state_now, parent_list, member, row_local, 1)
    second_out = outgoing(state_now, parent_list, member, row_local, 2)
    corner_out = outgoing(state_now, parent_list, member, row_local, 3)
    got_one = from_partner(first_out, "rows", 0)
    got_two = from_partner(second_out, "rows", 1)
    relayed = from_partner(corner_out, "rows", 0)
    got_three = from_partner(relayed, "rows", 1)
    own_list = lax.dynamic_slice_in_dim(parent_list, member * row_local, row_local, 0)
    source = own_list // row_local
    partner = jnp.bitwise_xor(source, member)
    slot_index = jnp.arange(row_local, dtype=jnp.int32)
    earlier = (source[:, None] == source[None, :]) & (slot_index[:, None] > slot_index[None, :])
    rank_index = jnp.sum(earlier.astype(jnp.int32), axis=1)
    position = jnp.where(
        partner == 0, own_list % row_local, row_local + (partner - 1) * CAP + rank_index
    )
    pooled = jnp.concatenate([state_now, got_one, got_two, got_three], 0)
    return jnp.take(pooled, position, axis=0)


def per_device(
    token_ids,
    parents,
    states,
    embed_table,
    qkv_weight,
    gate_weight,
    gate_bias,
    norm_gain,
    out_weight,
):
    row_local = states.shape[0]
    heads = states.shape[1]
    head_size = states.shape[2]
    count = lax.axis_size("rows")
    if (
        embed_table.shape[1] == head_size
        and head_size % 128 == 0
        and count == heads
        and parents.shape[0] == 1
        and parents.shape[2] == 4 * row_local
        and parents.shape[1] * 4 == count
        and row_local % 8 == 0
        and heads % 16 == 0
        and math.prod(embed_table.shape) * 2 <= 1 << 24
        and math.prod(states.shape) * 2 <= 1 << 23
    ):
        return fast(
            token_ids, parents, states, embed_table, qkv_weight, gate_weight, gate_bias,
            norm_gain, out_weight
        )
    width = heads * head_size
    column_local = embed_table.shape[1]
    row_total = token_ids.shape[1]
    device = lax.axis_index("rows")
    member = device % 4
    user_index = device // 4
    weight_flat = qkv_weight.reshape(qkv_weight.shape[0], 3 * column_local)
    local_columns = jnp.take(embed_table, token_ids, axis=0)
    every_proj = jnp.einsum(
        "...rc,cf->...rf",
        lax.all_gather(local_columns, "rows", axis=2, tiled=True),
        weight_flat,
        preferred_element_type=jnp.float32,
    )
    state_now = states
    step_proj = every_proj[0]
    projected = step_proj.astype(jnp.bfloat16).reshape(row_total, 3, column_local)
    mine = lax.all_to_all(projected, "rows", split_axis=0, concat_axis=2, tiled=True)
    queries = mine[:, 0].reshape(row_local, heads, head_size)
    key_float = mine[:, 1].reshape(row_local, heads, head_size).astype(jnp.float32)
    values = mine[:, 2].reshape(row_local, heads, head_size).astype(jnp.float32)
    gate_logit = jnp.sum(key_float * gate_weight, axis=-1) / math.sqrt(head_size) + gate_bias
    decay_rate = jax.nn.sigmoid(gate_logit)
    key_unit = key_float * lax.rsqrt(jnp.sum(key_float * key_float, axis=-1, keepdims=True) + 1e-06)
    parent_list = lax.dynamic_index_in_dim(parents[0], user_index, 0, keepdims=False)
    prior_state = route(state_now, parent_list, member, row_local)
    new_state = (
        decay_rate[:, :, None, None] * prior_state.astype(jnp.float32)
        + key_unit[:, :, :, None] * values[:, :, None, :]
    )
    state_now = new_state.astype(jnp.bfloat16)
    readout = jnp.einsum("rhd,rhde->rhe", queries, state_now, preferred_element_type=jnp.float32)
    scaled = readout * lax.rsqrt(jnp.mean(readout * readout, axis=-1, keepdims=True) + 1e-05)
    normed = (scaled.reshape(row_local, width) * norm_gain).astype(jnp.bfloat16)
    attention = jnp.dot(
        lax.all_gather(normed, "rows", axis=0, tiled=True),
        out_weight,
        preferred_element_type=jnp.float32,
    )
    outputs = [(local_columns[0].astype(jnp.float32) + attention).astype(jnp.bfloat16)]
    return (jnp.stack(outputs), state_now)


def solution(mesh):
    placed = (
        P(None, "groups"),
        P(None, "groups", None),
        P(("groups", "rows"), None, None, None),
        P(None, "rows"),
        P(None, None, "rows"),
        P(),
        P(),
        P(),
        P(None, "rows"),
    )
    return jax.shard_map(
        per_device,
        mesh=mesh,
        in_specs=placed,
        out_specs=(P(None, "groups", "rows"), P(("groups", "rows"), None, None, None)),
        check_vma=False,
    )
```

```python
import functools
import math

import jax
import jax.numpy as jnp
from jax import lax
from jax.experimental import pallas as pl
from jax.experimental.pallas import tpu as pltpu
from jax.sharding import PartitionSpec as P

CAP = 2
SPANS = (2, 5, 3, 6)
ANY = pl.BlockSpec(memory_space=pl.ANY)
VM = pl.BlockSpec(memory_space=pltpu.VMEM)
SM = pl.BlockSpec(memory_space=pltpu.SMEM)


def neighbours(count):
    me = lax.axis_index("rows")
    member, my_level = me % 4, me // 4
    side_member = (member + 2) % 4
    twin_member = member + 1 - 2 * (member % 2)
    diag_member = (twin_member + 2) % 4
    levels = [(my_level + k) % (count // 4) for k in range(1, count // 4)]
    return me, my_level, member, side_member, twin_member, diag_member, levels


def remote(source, target_ref, out_sem, in_sem, target):
    return pltpu.make_async_remote_copy(
        src_ref=source,
        dst_ref=target_ref,
        send_sem=out_sem,
        recv_sem=in_sem,
        device_id={"rows": target},
        device_id_type=pl.DeviceIdType.MESH,
    )


def across(row):
    size = row.shape[1]
    wide = jnp.broadcast_to(row, (size, size))
    here = lax.broadcasted_iota(jnp.int32, (size, size), 0)
    there = lax.broadcasted_iota(jnp.int32, (size, size), 1)
    return jnp.sum(jnp.where(here == there, wide, 0.0), axis=1, keepdims=True)


def layer_kernel(
    count, row_local, cuts, list_s, tok_s, bias_s, list_v, gate_v, gain_v, states, table, weights,
    out_weights, got, got_one, unit_o, value_o, decay_o, layer_o,
    first_heads, st, sb, tab, wts, owts, wide, rows_f, every, proj, qkv, units, vals, decs, spread, slots,
    normed, unit_v, value_v, decay_v, layer_v, layer_b,
    load_sem, tab_sem, w_sem, o_sem, send_sem, bulk_send, bulk_recv, recv_a, recv_b, recv_c,
    recv_d
):
    me, my_level, member, side_m, twin_m, diag_m, levels = neighbours(count)
    side, twin, diag = (my_level * 4 + m for m in (side_m, twin_m, diag_m))
    heads, head_size = st.shape[1], st.shape[2]
    beams = 4 * row_local
    half = member % 2

    barrier = pltpu.get_barrier_semaphore()
    peers = [side, twin, diag] + [other * 4 + member for other in levels]
    for peer in peers:
        pl.semaphore_signal(
            barrier, inc=1, device_id={"rows": peer}, device_id_type=pl.DeviceIdType.MESH
        )
    early = cuts[0][1]
    state_loads = [
        pltpu.make_async_copy(
            states.at[:, pl.ds(first, length)], into, load_sem.at[k]
        )
        for k, (first, length, into) in enumerate(
            ((0, early, first_heads), (0, heads, st))
        )
    ]
    pieces = tab_sem.shape[0]
    span = tab.shape[0] // pieces
    table_loads = [
        pltpu.make_async_copy(
            table.at[pl.ds(k * span, span)], tab.at[pl.ds(k * span, span)], tab_sem.at[k]
        )
        for k in range(pieces)
    ]
    weight_load = pltpu.make_async_copy(weights, wts, w_sem.at[0])
    out_load = pltpu.make_async_copy(out_weights, owts, w_sem.at[1])
    for load in state_loads[:1] + table_loads + state_loads[1:] + [weight_load, out_load]:
        load.start()

    chosen = []
    for partner in (2, 3, 1):
        target = (side_m, diag_m, twin_m)[(2, 3, 1).index(partner)]
        seen = jnp.int32(0)
        picks = [jnp.int32(0)] * CAP
        for child in range(row_local):
            parent = list_s[0, my_level, target * row_local + child]
            needed = lax.div(parent, row_local) == member
            for order in range(CAP):
                picks[order] = jnp.where(
                    needed & (seen == order), lax.rem(parent, row_local), picks[order]
                )
            seen = seen + needed.astype(jnp.int32)
        chosen += picks
    state_loads[0].wait()
    for slot in range(2 * CAP):
        sb[slot, :early] = first_heads[chosen[slot]]
    pl.semaphore_wait(barrier, len(peers))

    sent, arriving = [], []

    def bulk(index):
        first, length = cuts[index]
        for slot in range(2 * CAP):
            at = index * 2 * CAP + slot
            copy = remote(
                sb.at[slot, pl.ds(first, length)], got.at[slot, pl.ds(first, length)],
                bulk_send.at[at], bulk_recv.at[at], side if slot < CAP else diag,
            )
            copy.start()
            arriving.append(copy)

    def send(source, target_ref, sem, target):
        copy = remote(source, target_ref, send_sem.at[len(sent)], sem, target)
        copy.start()
        sent.append(copy)

    def arrived(ref, sem):
        remote(ref, ref, send_sem.at[0], sem, twin).wait_recv()

    bulk(0)
    for load in table_loads:
        load.wait()
    tokens = rows_f.shape[0]

    def fetch(i, carry):
        wide[pl.ds(pl.multiple_of(i * 8, 8), 8), :] = tab[lax.div(tok_s[0, i], 8)].astype(
            jnp.float32
        )
        return carry

    def pick(i, carry):
        rows_f[pl.ds(i, 1), :] = wide[pl.ds(i * 8 + lax.rem(tok_s[0, i], 8), 1), :]
        return carry

    lax.fori_loop(0, tokens, fetch, 0, unroll=8)
    lax.fori_loop(0, tokens, pick, 0, unroll=8)
    every[me] = rows_f[...].astype(jnp.bfloat16)

    mine = every.at[me]
    send(mine, mine, recv_a.at[me], side)
    for other in levels:
        send(mine, mine, recv_a.at[me], other * 4 + member)
    send(mine, mine, recv_a.at[me], twin)
    state_loads[1].wait()
    for slot in range(2 * CAP):
        sb[slot, early:] = st[chosen[slot], early:]
    for slot in range(2 * CAP, 3 * CAP):
        sb[slot] = st[chosen[slot]]
    bulk(1)

    def took(buffer, sems, block):
        arrived(buffer.at[block], sems.at[block])

    def forward(buffer, sems, block, target):
        send(buffer.at[block], buffer.at[block], sems.at[block], target)

    took(every, recv_a, side)
    for other in levels:
        forward(every, recv_a, side, other * 4 + member)
    forward(every, recv_a, side, twin)
    for column in (member, side_m):
        for other in levels:
            took(every, recv_a, other * 4 + column)
            forward(every, recv_a, other * 4 + column, twin)
    took(every, recv_a, twin)
    took(every, recv_a, diag)
    for column in (twin_m, diag_m):
        for other in levels:
            took(every, recv_a, other * 4 + column)

    weight_load.wait()
    lhs = jnp.concatenate([every[k] for k in range(count)], axis=1)
    for slab in range(3):
        done = jnp.dot(lhs, wts[slab], preferred_element_type=jnp.float32)
        done = done.astype(jnp.bfloat16)
        for level in range(count // 4):
            proj[level, :, slab * head_size : (slab + 1) * head_size] = done[
                level * beams : (level + 1) * beams
            ]

    own = proj.at[my_level]
    for other in levels:
        send(proj.at[other], qkv.at[me], recv_b.at[me], other * 4 + member)
    send(own, qkv.at[me], recv_b.at[me], side)
    send(own, qkv.at[me], recv_b.at[me], twin)
    qkv[me] = proj[my_level]
    for other in levels:
        took(qkv, recv_b, other * 4 + member)
        forward(qkv, recv_b, other * 4 + member, side)
        forward(qkv, recv_b, other * 4 + member, twin)
    bulk(2)
    for level in [my_level] + levels:
        took(qkv, recv_b, level * 4 + side_m)
        forward(qkv, recv_b, level * 4 + side_m, twin)

    lists = list_v[0, pl.ds(my_level, 1), :].astype(jnp.float32)
    place_row = lax.broadcasted_iota(jnp.int32, (1, beams), 1)
    place_col = lax.broadcasted_iota(jnp.int32, (beams, 1), 0)
    lists_row = lists.astype(jnp.int32)
    lists_col = across(lists).astype(jnp.int32)
    block_row, block_col = lax.div(place_row, row_local), lax.div(place_col, row_local)
    from_row, from_col = lax.div(lists_row, row_local), lax.div(lists_col, row_local)
    same = (block_row == block_col) & (from_row == from_col)
    rank_col = jnp.sum(
        jnp.where(same & (place_row < place_col), 1.0, 0.0), axis=1, keepdims=True
    ).astype(jnp.int32)
    rank_row = jnp.sum(
        jnp.where(same & (place_col < place_row), 1.0, 0.0), axis=0, keepdims=True
    ).astype(jnp.int32)
    off_row = jnp.bitwise_xor(block_row, from_row)
    off_col = jnp.bitwise_xor(block_col, from_col)
    slot_row = jnp.where(
        off_row == 0, lax.rem(place_row, row_local), row_local + (off_row - 1) * CAP + rank_row
    )
    slot_col = jnp.where(
        off_col == 0, lax.rem(place_col, row_local), row_local + (off_col - 1) * CAP + rank_col
    )
    slot_count = slots.shape[1]
    slot_index = lax.broadcasted_iota(jnp.int32, (slot_count, beams), 0)
    slot_pick = jnp.where(
        (from_row == member) & (slot_row == slot_index), 1.0, 0.0
    ).astype(jnp.bfloat16)
    wanted = from_col * slot_count + slot_col
    all_slots = lax.broadcasted_iota(jnp.int32, (beams, 4 * slot_count), 1)
    row_pick = jnp.where(wanted == all_slots, 1.0, 0.0)
    row_pick = jnp.concatenate(
        [
            row_pick[m * row_local : (m + 1) * row_local]
            for m in (0, 2, 1, 3)
        ],
        axis=0,
    ).astype(jnp.bfloat16)
    held = jnp.broadcast_to(from_col == member, (beams, head_size))
    within = jnp.broadcast_to(lax.rem(lists_col, row_local), (beams, head_size))
    masks = [held & (within == p) for p in range(row_local)]

    for column in (twin_m, diag_m):
        for level in [my_level] + levels:
            took(qkv, recv_b, level * 4 + column)
    for slot in range(CAP):
        copy = remote(
            sb.at[2 * CAP + slot], got_one.at[slot],
            bulk_send.at[len(cuts) * 2 * CAP + slot], bulk_recv.at[len(cuts) * 2 * CAP + slot],
            twin,
        )
        copy.start()
        arriving.append(copy)

    for head in range(heads):
        block = qkv[head]
        queries = block[:, :head_size].astype(jnp.float32)
        keys = block[:, head_size : 2 * head_size].astype(jnp.float32)
        values = block[:, 2 * head_size :].astype(jnp.float32)
        logit = jnp.sum(keys * gate_v[head : head + 1], axis=-1, keepdims=True)
        decay = jax.nn.sigmoid(logit / math.sqrt(head_size) + bias_s[head])
        unit = keys * lax.rsqrt(jnp.sum(keys * keys, axis=-1, keepdims=True) + 1e-06)
        spreadq = jnp.concatenate(
            [jnp.where(mask, queries, 0.0).astype(jnp.bfloat16) for mask in masks], axis=1
        )
        stacked = st[:, head].reshape(row_local * head_size, head_size)
        total = jnp.dot(spreadq, stacked, preferred_element_type=jnp.float32)
        readout = decay * total + jnp.sum(queries * unit, axis=-1, keepdims=True) * values
        scaled = readout * lax.rsqrt(jnp.mean(readout * readout, axis=-1, keepdims=True) + 1e-05)
        spread[:, head * head_size : (head + 1) * head_size] = (
            scaled * gain_v[head : head + 1]
        ).astype(jnp.bfloat16)
        units[head] = unit
        vals[head] = values
        decs[head] = jnp.broadcast_to(decay, (beams, head_size))
    slots[member] = jnp.dot(
        slot_pick, spread[...], preferred_element_type=jnp.float32
    ).astype(jnp.bfloat16)

    forward(slots, recv_c, member, side)
    forward(slots, recv_c, member, twin)
    bulk(3)
    for head in range(heads):
        here = pl.ds(pl.multiple_of(member * row_local, row_local), row_local)
        for target, source in ((unit_v, units), (value_v, vals), (decay_v, decs)):
            target[:, head : head + 1, :] = source[head, here, :].reshape(
                row_local, 1, head_size
            )
    took(slots, recv_c, side_m)
    forward(slots, recv_c, side_m, twin)
    took(slots, recv_c, twin_m)
    took(slots, recv_c, diag_m)
    level_rows = jnp.dot(
        row_pick, slots[...].reshape(4 * slot_count, heads * head_size),
        preferred_element_type=jnp.float32,
    ).astype(jnp.bfloat16)
    for core in range(2):
        normed[my_level * 2 + core] = level_rows[core * 2 * row_local : (core + 1) * 2 * row_local]
    for other in levels:
        forward(normed, recv_d, my_level * 2 + half, other * 4 + member)
    for other in levels:
        took(normed, recv_d, other * 2 + half)
        forward(normed, recv_d, other * 2 + half, twin)
    for other in levels:
        took(normed, recv_d, other * 2 + 1 - half)
    out_load.wait()
    attention = jnp.dot(
        normed[...].reshape(count * row_local, heads * head_size), owts[...],
        preferred_element_type=jnp.float32,
    )
    for level in range(count // 4):
        for core in range(2):
            for line in range(2):
                source = ((level * 2 + core) * 2 + line) * row_local
                target = ((level * 2 + line) * 2 + core) * row_local
                rows = slice(target, target + row_local)
                layer_v[rows] = rows_f[rows] + attention[source : source + row_local]
    layer_b[...] = layer_v[...].astype(jnp.bfloat16)
    outs = [
        pltpu.make_async_copy(source, target, o_sem.at[k])
        for k, (source, target) in enumerate(
            (
                (unit_v, unit_o), (value_v, value_o), (decay_v, decay_o), (layer_b, layer_o)
            )
        )
    ]
    for copy in sent:
        copy.wait_send()
    for copy in outs:
        copy.start()
    for copy in arriving:
        copy.wait()
    for copy in outs:
        copy.wait()


def layer(
    parents, tokens, gate_bias, gate_weight, norm_gain, states, table, weights, out_weight, count
):
    row_local, heads, head_size, _ = states.shape
    row_total, depth = tokens.shape[1], weights.shape[1]
    beams = parents.shape[2]
    slot_count = 16 * ((row_local + 3 * CAP + 15) // 16)
    cuts, first = [], 0
    for span in SPANS:
        cuts.append((first, span * heads // 16))
        first += span * heads // 16
    bulk = (len(cuts) * 2 + 1) * CAP
    sends = 64
    bf, f32 = jnp.bfloat16, jnp.float32
    dma = pltpu.SemaphoreType.DMA
    rows = (row_local, heads, head_size)
    return pl.pallas_call(
        functools.partial(layer_kernel, count, row_local, tuple(cuts)),
        out_shape=(
            jax.ShapeDtypeStruct((2 * CAP,) + states.shape[1:], states.dtype),
            jax.ShapeDtypeStruct((CAP,) + states.shape[1:], states.dtype),
            jax.ShapeDtypeStruct(rows, f32),
            jax.ShapeDtypeStruct(rows, f32),
            jax.ShapeDtypeStruct(rows, f32),
            jax.ShapeDtypeStruct((row_total, head_size), bf),
        ),
        in_specs=[SM, SM, SM, VM, VM, VM, ANY, ANY, ANY, ANY],
        out_specs=(ANY,) * 6,
        scratch_shapes=[
            pltpu.VMEM((row_local, cuts[0][1]) + states.shape[2:], bf),
            pltpu.VMEM(states.shape, bf),
            pltpu.VMEM((3 * CAP,) + states.shape[1:], bf),
            pltpu.VMEM((table.shape[0] // 8, 8, head_size), bf),
            pltpu.VMEM(weights.shape, bf),
            pltpu.VMEM(out_weight.shape, bf),
            pltpu.VMEM((row_total * 8, head_size), f32),
            pltpu.VMEM((row_total, head_size), f32),
            pltpu.VMEM((count, row_total, head_size), bf),
            pltpu.VMEM((count // 4, beams, 3 * head_size), bf),
            pltpu.VMEM((count, beams, 3 * head_size), bf),
            pltpu.VMEM((heads, beams, head_size), f32),
            pltpu.VMEM((heads, beams, head_size), f32),
            pltpu.VMEM((heads, beams, head_size), f32),
            pltpu.VMEM((beams, heads * head_size), bf),
            pltpu.VMEM((4, slot_count, heads * head_size), bf),
            pltpu.VMEM((count // 2, 2 * row_local, heads * head_size), bf),
            pltpu.VMEM(rows, f32),
            pltpu.VMEM(rows, f32),
            pltpu.VMEM(rows, f32),
            pltpu.VMEM((row_total, head_size), f32),
            pltpu.VMEM((row_total, head_size), bf),
            dma((2,)),
            dma((4,)),
            dma((2,)),
            dma((4,)),
            dma((sends,)),
            dma((bulk,)),
            dma((bulk,)),
            dma((count,)),
            dma((count,)),
            dma((4,)),
            dma((count // 2,)),
        ],
        compiler_params=pltpu.CompilerParams(collective_id=1, has_side_effects=True),
        name="layer_step",
    )(
        parents, tokens, gate_bias, parents, gate_weight, norm_gain.reshape(heads, head_size),
        states, table.reshape(table.shape[0] // 8, 8, head_size), weights, out_weight,
    )


def update_kernel(
    list_s, states, got, got_one, units, values, decays, layer_in, out_ref, layer_out,
    old, new, unit_v, value_v, decay_v, layer_v, in_sem, out_sem, side_sem
):
    row_local, heads = old.shape[0], old.shape[1]
    device = lax.axis_index("rows")
    member, user = device % 4, device // 4
    sides = [
        pltpu.make_async_copy(source, target, side_sem.at[k])
        for k, (source, target) in enumerate(
            ((units, unit_v), (values, value_v), (decays, decay_v), (layer_in, layer_v))
        )
    ]
    for copy in sides:
        copy.start()
    parents = [list_s[0, user, member * row_local + row] for row in range(row_local)]
    blocks = [lax.div(parent, row_local) for parent in parents]
    for row in range(row_local):
        partner = jnp.bitwise_xor(blocks[row], member)
        rank = jnp.int32(0)
        for earlier in range(row):
            rank = rank + (blocks[earlier] == blocks[row]).astype(jnp.int32)

        @pl.when(partner == 0)
        def _():
            pltpu.make_async_copy(
                states.at[lax.rem(parents[row], row_local)], old.at[row], in_sem.at[row]
            ).start()

        @pl.when(partner == 1)
        def _():
            pltpu.make_async_copy(got_one.at[rank], old.at[row], in_sem.at[row]).start()

        @pl.when(partner > 1)
        def _():
            pltpu.make_async_copy(
                got.at[(partner - 2) * CAP + rank], old.at[row], in_sem.at[row]
            ).start()

    for copy in sides:
        copy.wait()
    last = pltpu.make_async_copy(layer_v, layer_out, side_sem.at[0])
    last.start()

    def step(row, carry):
        pltpu.make_async_copy(states.at[0], old.at[row], in_sem.at[row]).wait()
        columns = jnp.transpose(unit_v[row])
        value = value_v[row]
        decay = decay_v[row]
        for head in range(heads):
            fresh = columns[:, head : head + 1] * value[head : head + 1, :]
            prior = old[row, head].astype(jnp.float32)
            new[row, head] = (decay[head : head + 1, :] * prior + fresh).astype(jnp.bfloat16)
        pltpu.make_async_copy(new.at[row], out_ref.at[row], out_sem.at[row]).start()
        return carry

    lax.fori_loop(0, row_local, step, 0)
    for row in range(row_local):
        pltpu.make_async_copy(new.at[row], out_ref.at[row], out_sem.at[row]).wait()
    last.wait()


def update(parents, states, got, got_one, units, values, decays, layer_in):
    row_local = states.shape[0]
    return pl.pallas_call(
        update_kernel,
        out_shape=(
            jax.ShapeDtypeStruct(states.shape, states.dtype),
            jax.ShapeDtypeStruct(layer_in.shape, layer_in.dtype),
        ),
        in_specs=[SM] + [ANY] * 7,
        out_specs=(ANY, ANY),
        scratch_shapes=[
            pltpu.VMEM(states.shape, states.dtype),
            pltpu.VMEM(states.shape, states.dtype),
            pltpu.VMEM(units.shape, units.dtype),
            pltpu.VMEM(values.shape, values.dtype),
            pltpu.VMEM(decays.shape, decays.dtype),
            pltpu.VMEM(layer_in.shape, layer_in.dtype),
            pltpu.SemaphoreType.DMA((row_local,)),
            pltpu.SemaphoreType.DMA((row_local,)),
            pltpu.SemaphoreType.DMA((4,)),
        ],
        cost_estimate=pl.CostEstimate(
            flops=4 * math.prod(states.shape),
            bytes_accessed=4 * math.prod(states.shape),
            transcendentals=0,
        ),
        name="update_states",
    )(parents, states, got, got_one, units, values, decays, layer_in)


def fast(
    token_ids, parents, states, embed_table, qkv_weight, gate_weight, gate_bias, norm_gain,
    out_weight
):
    count = lax.axis_size("rows")
    got, got_one, units, values, decays, layer_mid = layer(
        parents, token_ids, gate_bias, gate_weight, norm_gain, states, embed_table,
        jnp.transpose(qkv_weight, (1, 0, 2)), out_weight, count,
    )
    state_now, layer_out = update(
        parents, states, got, got_one, units, values, decays, layer_mid
    )
    return (layer_out[None], state_now)


def from_partner(block, axis, stride):
    count = lax.axis_size(axis)
    route = []
    for low in range(count):
        high = low | 1 << stride
        if high != low and high < count:
            route += [(low, high), (high, low)]
    return lax.ppermute(block, axis, route)


def outgoing(state_now, parent_list, member, row_local, partner):
    target = jnp.bitwise_xor(member, partner)
    children = lax.dynamic_slice_in_dim(parent_list, target * row_local, row_local, 0)
    needed = children // row_local == member
    rank_index = jnp.cumsum(needed.astype(jnp.int32)) - 1
    slot_ids = jnp.arange(CAP, dtype=jnp.int32)
    chosen = jnp.sum(
        jnp.where(
            needed[None, :] & (rank_index[None, :] == slot_ids[:, None]),
            (children % row_local)[None, :],
            0,
        ),
        axis=1,
    )
    return jnp.take(state_now, chosen, axis=0)


def route(state_now, parent_list, member, row_local):
    first_out = outgoing(state_now, parent_list, member, row_local, 1)
    second_out = outgoing(state_now, parent_list, member, row_local, 2)
    corner_out = outgoing(state_now, parent_list, member, row_local, 3)
    got_one = from_partner(first_out, "rows", 0)
    got_two = from_partner(second_out, "rows", 1)
    relayed = from_partner(corner_out, "rows", 0)
    got_three = from_partner(relayed, "rows", 1)
    own_list = lax.dynamic_slice_in_dim(parent_list, member * row_local, row_local, 0)
    source = own_list // row_local
    partner = jnp.bitwise_xor(source, member)
    slot_index = jnp.arange(row_local, dtype=jnp.int32)
    earlier = (source[:, None] == source[None, :]) & (slot_index[:, None] > slot_index[None, :])
    rank_index = jnp.sum(earlier.astype(jnp.int32), axis=1)
    position = jnp.where(
        partner == 0, own_list % row_local, row_local + (partner - 1) * CAP + rank_index
    )
    pooled = jnp.concatenate([state_now, got_one, got_two, got_three], 0)
    return jnp.take(pooled, position, axis=0)


def per_device(
    token_ids,
    parents,
    states,
    embed_table,
    qkv_weight,
    gate_weight,
    gate_bias,
    norm_gain,
    out_weight,
):
    row_local = states.shape[0]
    heads = states.shape[1]
    head_size = states.shape[2]
    count = lax.axis_size("rows")
    if (
        embed_table.shape[1] == head_size
        and head_size % 128 == 0
        and count == heads
        and parents.shape[0] == 1
        and parents.shape[2] == 4 * row_local
        and parents.shape[1] * 4 == count
        and row_local % 8 == 0
        and heads % 16 == 0
        and math.prod(embed_table.shape) * 2 <= 1 << 24
        and math.prod(states.shape) * 2 <= 1 << 23
    ):
        return fast(
            token_ids, parents, states, embed_table, qkv_weight, gate_weight, gate_bias,
            norm_gain, out_weight
        )
    width = heads * head_size
    column_local = embed_table.shape[1]
    row_total = token_ids.shape[1]
    device = lax.axis_index("rows")
    member = device % 4
    user_index = device // 4
    weight_flat = qkv_weight.reshape(qkv_weight.shape[0], 3 * column_local)
    local_columns = jnp.take(embed_table, token_ids, axis=0)
    every_proj = jnp.einsum(
        "...rc,cf->...rf",
        lax.all_gather(local_columns, "rows", axis=2, tiled=True),
        weight_flat,
        preferred_element_type=jnp.float32,
    )
    state_now = states
    step_proj = every_proj[0]
    projected = step_proj.astype(jnp.bfloat16).reshape(row_total, 3, column_local)
    mine = lax.all_to_all(projected, "rows", split_axis=0, concat_axis=2, tiled=True)
    queries = mine[:, 0].reshape(row_local, heads, head_size)
    key_float = mine[:, 1].reshape(row_local, heads, head_size).astype(jnp.float32)
    values = mine[:, 2].reshape(row_local, heads, head_size).astype(jnp.float32)
    gate_logit = jnp.sum(key_float * gate_weight, axis=-1) / math.sqrt(head_size) + gate_bias
    decay_rate = jax.nn.sigmoid(gate_logit)
    key_unit = key_float * lax.rsqrt(jnp.sum(key_float * key_float, axis=-1, keepdims=True) + 1e-06)
    parent_list = lax.dynamic_index_in_dim(parents[0], user_index, 0, keepdims=False)
    prior_state = route(state_now, parent_list, member, row_local)
    new_state = (
        decay_rate[:, :, None, None] * prior_state.astype(jnp.float32)
        + key_unit[:, :, :, None] * values[:, :, None, :]
    )
    state_now = new_state.astype(jnp.bfloat16)
    readout = jnp.einsum("rhd,rhde->rhe", queries, state_now, preferred_element_type=jnp.float32)
    scaled = readout * lax.rsqrt(jnp.mean(readout * readout, axis=-1, keepdims=True) + 1e-05)
    normed = (scaled.reshape(row_local, width) * norm_gain).astype(jnp.bfloat16)
    attention = jnp.dot(
        lax.all_gather(normed, "rows", axis=0, tiled=True),
        out_weight,
        preferred_element_type=jnp.float32,
    )
    outputs = [(local_columns[0].astype(jnp.float32) + attention).astype(jnp.bfloat16)]
    return (jnp.stack(outputs), state_now)


def solution(mesh):
    placed = (
        P(None, "groups"),
        P(None, "groups", None),
        P(("groups", "rows"), None, None, None),
        P(None, "rows"),
        P(None, None, "rows"),
        P(),
        P(),
        P(),
        P(None, "rows"),
    )
    return jax.shard_map(
        per_device,
        mesh=mesh,
        in_specs=placed,
        out_specs=(P(None, "groups", "rows"), P(("groups", "rows"), None, None, None)),
        check_vma=False,
    )
```

```python
import functools
import math

import jax
import jax.numpy as jnp
from jax import lax
from jax.experimental import pallas as pl
from jax.experimental.pallas import tpu as pltpu
from jax.sharding import PartitionSpec as P

CAP = 2
SPANS = (2, 5, 3, 3, 3)
LAYER_VMEM, UPDATE_VMEM = 44 << 20, 8 << 20
ANY = pl.BlockSpec(memory_space=pl.ANY)
VM = pl.BlockSpec(memory_space=pltpu.VMEM)
SM = pl.BlockSpec(memory_space=pltpu.SMEM)


def neighbours(count):
    me = lax.axis_index("rows")
    member, my_level = me % 4, me // 4
    side_member = (member + 2) % 4
    twin_member = member + 1 - 2 * (member % 2)
    diag_member = (twin_member + 2) % 4
    levels = [(my_level + k) % (count // 4) for k in range(1, count // 4)]
    return me, my_level, member, side_member, twin_member, diag_member, levels


def remote(source, target_ref, out_sem, in_sem, target):
    return pltpu.make_async_remote_copy(
        src_ref=source,
        dst_ref=target_ref,
        send_sem=out_sem,
        recv_sem=in_sem,
        device_id={"rows": target},
        device_id_type=pl.DeviceIdType.MESH,
    )


def across(row):
    size = row.shape[1]
    wide = jnp.broadcast_to(row, (size, size))
    here = lax.broadcasted_iota(jnp.int32, (size, size), 0)
    there = lax.broadcasted_iota(jnp.int32, (size, size), 1)
    return jnp.sum(jnp.where(here == there, wide, 0.0), axis=1, keepdims=True)


def layer_kernel(
    count, row_local, cuts, list_s, tok_s, bias_s, list_v, gate_v, gain_v, states, table, weights,
    out_weights, new_o, late_o, unit_v, value_v, decay_v, layer_o,
    first_heads, pool, one_v, sb, tab, wts, owts, wide, rows_f, every, proj, qkv, units, vals,
    decs, spread, slots, normed, layer_v,
    load_sem, tab_sem, w_sem, send_sem, bulk_send, bulk_recv, recv_a, recv_b, recv_c, recv_d,
    *got
):
    got = list(got) + [late_o]
    me, my_level, member, side_m, twin_m, diag_m, levels = neighbours(count)
    side, twin, diag = (my_level * 4 + m for m in (side_m, twin_m, diag_m))
    heads, head_size = pool.shape[1], pool.shape[2]
    st = pool.at[pl.ds(0, row_local)]
    beams = 4 * row_local
    half = member % 2

    barrier = pltpu.get_barrier_semaphore()
    peers = [side, twin, diag] + [other * 4 + member for other in levels]
    for peer in peers:
        pl.semaphore_signal(
            barrier, inc=1, device_id={"rows": peer}, device_id_type=pl.DeviceIdType.MESH
        )
    early = cuts[0][1]
    state_loads = [
        pltpu.make_async_copy(
            states.at[:, pl.ds(first, length)], into, load_sem.at[k]
        )
        for k, (first, length, into) in enumerate(
            ((0, early, first_heads), (0, heads, st))
        )
    ]
    pieces = tab_sem.shape[0]
    span = tab.shape[0] // pieces
    table_loads = [
        pltpu.make_async_copy(
            table.at[pl.ds(k * span, span)], tab.at[pl.ds(k * span, span)], tab_sem.at[k]
        )
        for k in range(pieces)
    ]
    weight_load = pltpu.make_async_copy(weights, wts, w_sem.at[0])
    out_load = pltpu.make_async_copy(out_weights, owts, w_sem.at[1])
    for load in state_loads[:1] + table_loads + state_loads[1:] + [weight_load, out_load]:
        load.start()

    chosen = []
    for partner in (2, 3, 1):
        target = (side_m, diag_m, twin_m)[(2, 3, 1).index(partner)]
        seen = jnp.int32(0)
        picks = [jnp.int32(0)] * CAP
        for child in range(row_local):
            parent = list_s[0, my_level, target * row_local + child]
            needed = lax.div(parent, row_local) == member
            for order in range(CAP):
                picks[order] = jnp.where(
                    needed & (seen == order), lax.rem(parent, row_local), picks[order]
                )
            seen = seen + needed.astype(jnp.int32)
        chosen += picks
    state_loads[0].wait()
    for slot in range(2 * CAP):
        sb[slot, :early] = first_heads[chosen[slot]]
    pl.semaphore_wait(barrier, len(peers))

    sent, arriving, twin_copies = [], [[] for _ in cuts], []

    def bulk(index):
        first, length = cuts[index]
        for slot in range(2 * CAP):
            at = index * 2 * CAP + slot
            copy = remote(
                sb.at[slot, pl.ds(first, length)], got[index].at[slot],
                bulk_send.at[at], bulk_recv.at[at], side if slot < CAP else diag,
            )
            copy.start()
            arriving[index].append(copy)

    def send(source, target_ref, sem, target):
        copy = remote(source, target_ref, send_sem.at[len(sent)], sem, target)
        copy.start()
        sent.append(copy)

    def arrived(ref, sem):
        remote(ref, ref, send_sem.at[0], sem, twin).wait_recv()

    bulk(0)
    for load in table_loads:
        load.wait()
    tokens = rows_f.shape[0]

    def fetch(i, carry):
        wide[pl.ds(pl.multiple_of(i * 8, 8), 8), :] = tab[lax.div(tok_s[0, i], 8)].astype(
            jnp.float32
        )
        return carry

    def pick(i, carry):
        rows_f[pl.ds(i, 1), :] = wide[pl.ds(i * 8 + lax.rem(tok_s[0, i], 8), 1), :]
        return carry

    lax.fori_loop(0, tokens, fetch, 0, unroll=8)
    lax.fori_loop(0, tokens, pick, 0, unroll=8)
    every[me] = rows_f[...].astype(jnp.bfloat16)

    mine = every.at[me]
    send(mine, mine, recv_a.at[me], side)
    for other in levels:
        send(mine, mine, recv_a.at[me], other * 4 + member)
    send(mine, mine, recv_a.at[me], twin)
    state_loads[1].wait()
    for slot in range(2 * CAP):
        sb[slot, early:] = pool[chosen[slot], early:]
    for slot in range(2 * CAP, 3 * CAP):
        sb[slot] = pool[chosen[slot]]
    bulk(1)

    def took(buffer, sems, block):
        arrived(buffer.at[block], sems.at[block])

    def forward(buffer, sems, block, target):
        send(buffer.at[block], buffer.at[block], sems.at[block], target)

    took(every, recv_a, side)
    for other in levels:
        forward(every, recv_a, side, other * 4 + member)
    forward(every, recv_a, side, twin)
    for column in (member, side_m):
        for other in levels:
            took(every, recv_a, other * 4 + column)
            forward(every, recv_a, other * 4 + column, twin)
    took(every, recv_a, twin)
    took(every, recv_a, diag)
    for column in (twin_m, diag_m):
        for other in levels:
            took(every, recv_a, other * 4 + column)

    weight_load.wait()
    lhs = jnp.concatenate([every[k] for k in range(count)], axis=1)
    for slab in range(3):
        done = jnp.dot(lhs, wts[slab], preferred_element_type=jnp.float32)
        done = done.astype(jnp.bfloat16)
        for level in range(count // 4):
            proj[level, :, slab * head_size : (slab + 1) * head_size] = done[
                level * beams : (level + 1) * beams
            ]

    own = proj.at[my_level]
    for other in levels:
        send(proj.at[other], qkv.at[me], recv_b.at[me], other * 4 + member)
    send(own, qkv.at[me], recv_b.at[me], side)
    send(own, qkv.at[me], recv_b.at[me], twin)
    qkv[me] = proj[my_level]
    for other in levels:
        took(qkv, recv_b, other * 4 + member)
        forward(qkv, recv_b, other * 4 + member, side)
        forward(qkv, recv_b, other * 4 + member, twin)
    bulk(2)
    for level in [my_level] + levels:
        took(qkv, recv_b, level * 4 + side_m)
        forward(qkv, recv_b, level * 4 + side_m, twin)

    lists = list_v[0, pl.ds(my_level, 1), :].astype(jnp.float32)
    place_row = lax.broadcasted_iota(jnp.int32, (1, beams), 1)
    place_col = lax.broadcasted_iota(jnp.int32, (beams, 1), 0)
    lists_row = lists.astype(jnp.int32)
    lists_col = across(lists).astype(jnp.int32)
    block_row, block_col = lax.div(place_row, row_local), lax.div(place_col, row_local)
    from_row, from_col = lax.div(lists_row, row_local), lax.div(lists_col, row_local)
    same = (block_row == block_col) & (from_row == from_col)
    rank_col = jnp.sum(
        jnp.where(same & (place_row < place_col), 1.0, 0.0), axis=1, keepdims=True
    ).astype(jnp.int32)
    rank_row = jnp.sum(
        jnp.where(same & (place_col < place_row), 1.0, 0.0), axis=0, keepdims=True
    ).astype(jnp.int32)
    off_row = jnp.bitwise_xor(block_row, from_row)
    off_col = jnp.bitwise_xor(block_col, from_col)
    slot_row = jnp.where(
        off_row == 0, lax.rem(place_row, row_local), row_local + (off_row - 1) * CAP + rank_row
    )
    slot_col = jnp.where(
        off_col == 0, lax.rem(place_col, row_local), row_local + (off_col - 1) * CAP + rank_col
    )
    slot_count = slots.shape[1]
    slot_index = lax.broadcasted_iota(jnp.int32, (slot_count, beams), 0)
    slot_pick = jnp.where(
        (from_row == member) & (slot_row == slot_index), 1.0, 0.0
    ).astype(jnp.bfloat16)
    wanted = from_col * slot_count + slot_col
    all_slots = lax.broadcasted_iota(jnp.int32, (beams, 4 * slot_count), 1)
    row_pick = jnp.where(wanted == all_slots, 1.0, 0.0)
    row_pick = jnp.concatenate(
        [
            row_pick[m * row_local : (m + 1) * row_local]
            for m in (0, 2, 1, 3)
        ],
        axis=0,
    ).astype(jnp.bfloat16)
    held = jnp.broadcast_to(from_col == member, (beams, head_size))
    within = jnp.broadcast_to(lax.rem(lists_col, row_local), (beams, head_size))
    masks = [held & (within == p) for p in range(row_local)]

    for column in (twin_m, diag_m):
        for level in [my_level] + levels:
            took(qkv, recv_b, level * 4 + column)
    for slot in range(CAP):
        copy = remote(
            sb.at[2 * CAP + slot], one_v.at[slot],
            bulk_send.at[len(cuts) * 2 * CAP + slot], bulk_recv.at[len(cuts) * 2 * CAP + slot],
            twin,
        )
        copy.start()
        twin_copies.append(copy)

    for head in range(heads):
        block = qkv[head]
        queries = block[:, :head_size].astype(jnp.float32)
        keys = block[:, head_size : 2 * head_size].astype(jnp.float32)
        values = block[:, 2 * head_size :].astype(jnp.float32)
        logit = jnp.sum(keys * gate_v[head : head + 1], axis=-1, keepdims=True)
        decay = jax.nn.sigmoid(logit / math.sqrt(head_size) + bias_s[head])
        unit = keys * lax.rsqrt(jnp.sum(keys * keys, axis=-1, keepdims=True) + 1e-06)
        spreadq = jnp.concatenate(
            [jnp.where(mask, queries, 0.0).astype(jnp.bfloat16) for mask in masks], axis=1
        )
        stacked = pool[:row_local, head].reshape(row_local * head_size, head_size)
        total = jnp.dot(spreadq, stacked, preferred_element_type=jnp.float32)
        readout = decay * total + jnp.sum(queries * unit, axis=-1, keepdims=True) * values
        scaled = readout * lax.rsqrt(jnp.mean(readout * readout, axis=-1, keepdims=True) + 1e-05)
        spread[:, head * head_size : (head + 1) * head_size] = (
            scaled * gain_v[head : head + 1]
        ).astype(jnp.bfloat16)
        units[head] = unit
        vals[head] = values
        decs[head] = jnp.broadcast_to(decay, (beams, head_size))
    slots[member] = jnp.dot(
        slot_pick, spread[...], preferred_element_type=jnp.float32
    ).astype(jnp.bfloat16)

    forward(slots, recv_c, member, side)
    forward(slots, recv_c, member, twin)
    for index in range(3, len(cuts)):
        bulk(index)
    for head in range(heads):
        here = pl.ds(pl.multiple_of(member * row_local, row_local), row_local)
        for target, source in ((unit_v, units), (value_v, vals), (decay_v, decs)):
            target[:, head : head + 1, :] = source[head, here, :].reshape(
                row_local, 1, head_size
            )
    took(slots, recv_c, side_m)
    forward(slots, recv_c, side_m, twin)
    took(slots, recv_c, twin_m)
    took(slots, recv_c, diag_m)
    level_rows = jnp.dot(
        row_pick, slots[...].reshape(4 * slot_count, heads * head_size),
        preferred_element_type=jnp.float32,
    ).astype(jnp.bfloat16)
    for core in range(2):
        normed[my_level * 2 + core] = level_rows[core * 2 * row_local : (core + 1) * 2 * row_local]
    for other in levels:
        forward(normed, recv_d, my_level * 2 + half, other * 4 + member)

    def collect(index):
        first, length = cuts[index]
        for copy in arriving[index]:
            copy.wait_recv()
        for slot in range(2 * CAP):
            pool[row_local + CAP + slot, first : first + length] = got[index][slot]

    def advance(first, last, late):
        def step(row, carry):
            base = member * row_local
            parent = list_s[0, my_level, base + row]
            block = lax.div(parent, row_local)
            rank = jnp.int32(0)
            for earlier in range(row_local):
                other = lax.div(list_s[0, my_level, base + earlier], row_local)
                rank = rank + ((other == block) & (earlier < row)).astype(jnp.int32)
            partner = jnp.bitwise_xor(block, member)
            rank = jnp.minimum(rank, CAP - 1)
            source = jnp.where(
                partner == 0, lax.rem(parent, row_local), row_local + (partner - 1) * CAP + rank
            )
            if late:
                source = jnp.where(partner > 1, 0, source)
            columns = jnp.transpose(unit_v[row])
            value, decay = value_v[row], decay_v[row]
            for head in range(first, last):
                fresh = columns[:, head : head + 1] * value[head : head + 1, :]
                prior = pool[source, head].astype(jnp.float32)
                new_o[row, head] = (decay[head : head + 1, :] * prior + fresh).astype(
                    jnp.bfloat16
                )
            return carry

        lax.fori_loop(0, row_local, step, 0)

    for copy in twin_copies:
        copy.wait_recv()
    for slot in range(CAP):
        pool[row_local + slot] = one_v[slot]
    for index in range(2):
        collect(index)
    advance(0, cuts[2][0], False)
    for other in levels:
        took(normed, recv_d, other * 2 + half)
        forward(normed, recv_d, other * 2 + half, twin)
    for other in levels:
        took(normed, recv_d, other * 2 + 1 - half)
    out_load.wait()
    attention = jnp.dot(
        normed[...].reshape(count * row_local, heads * head_size), owts[...],
        preferred_element_type=jnp.float32,
    )
    for level in range(count // 4):
        for core in range(2):
            for line in range(2):
                source = ((level * 2 + core) * 2 + line) * row_local
                target = ((level * 2 + line) * 2 + core) * row_local
                rows = slice(target, target + row_local)
                layer_v[rows] = rows_f[rows] + attention[source : source + row_local]
    layer_o[...] = layer_v[...].astype(jnp.bfloat16)
    late = cuts[-1][0]
    advance(late, heads, True)
    for index in range(2, len(cuts) - 1):
        collect(index)
        advance(cuts[index][0], cuts[index + 1][0], False)
    for copy in sent + twin_copies:
        copy.wait_send()
    for copies in arriving:
        for copy in copies:
            copy.wait_send()
    for copy in arriving[-1]:
        copy.wait_recv()


def layer(
    parents, tokens, gate_bias, gate_weight, norm_gain, states, table, weights, out_weight, count
):
    row_local, heads, head_size, _ = states.shape
    row_total, depth = tokens.shape[1], weights.shape[1]
    beams = parents.shape[2]
    slot_count = 16 * ((row_local + 3 * CAP + 15) // 16)
    cuts, first = [], 0
    for span in SPANS:
        cuts.append((first, span * heads // 16))
        first += span * heads // 16
    bulk = (len(cuts) * 2 + 1) * CAP
    sends = 64
    bf, f32 = jnp.bfloat16, jnp.float32
    dma = pltpu.SemaphoreType.DMA
    rows = (row_local, heads, head_size)
    whole = states.shape[1:]
    pool_rows = row_local + 3 * CAP

    def pieces(index):
        return (2 * CAP, cuts[index][1]) + states.shape[2:]

    return pl.pallas_call(
        functools.partial(layer_kernel, count, row_local, tuple(cuts)),
        out_shape=(
            pltpu.VMEM(states.shape, bf),
            pltpu.VMEM(pieces(-1), bf),
            pltpu.VMEM(rows, f32),
            pltpu.VMEM(rows, f32),
            pltpu.VMEM(rows, f32),
            pltpu.VMEM((row_total, head_size), bf),
        ),
        in_specs=[SM, SM, SM, VM, VM, VM, ANY, ANY, ANY, ANY],
        out_specs=(VM,) * 6,
        scratch_shapes=[
            pltpu.VMEM((row_local, cuts[0][1]) + states.shape[2:], bf),
            pltpu.VMEM((pool_rows,) + whole, bf),
            pltpu.VMEM((CAP,) + whole, bf),
            pltpu.VMEM((3 * CAP,) + whole, bf),
            pltpu.VMEM((table.shape[0] // 8, 8, head_size), bf),
            pltpu.VMEM(weights.shape, bf),
            pltpu.VMEM(out_weight.shape, bf),
            pltpu.VMEM((row_total * 8, head_size), f32),
            pltpu.VMEM((row_total, head_size), f32),
            pltpu.VMEM((count, row_total, head_size), bf),
            pltpu.VMEM((count // 4, beams, 3 * head_size), bf),
            pltpu.VMEM((count, beams, 3 * head_size), bf),
            pltpu.VMEM((heads, beams, head_size), f32),
            pltpu.VMEM((heads, beams, head_size), f32),
            pltpu.VMEM((heads, beams, head_size), f32),
            pltpu.VMEM((beams, heads * head_size), bf),
            pltpu.VMEM((4, slot_count, heads * head_size), bf),
            pltpu.VMEM((count // 2, 2 * row_local, heads * head_size), bf),
            pltpu.VMEM((row_total, head_size), f32),
            dma((2,)),
            dma((4,)),
            dma((2,)),
            dma((sends,)),
            dma((bulk,)),
            dma((bulk,)),
            dma((count,)),
            dma((count,)),
            dma((4,)),
            dma((count // 2,)),
        ]
        + [pltpu.VMEM(pieces(index), bf) for index in range(len(cuts) - 1)],
        compiler_params=pltpu.CompilerParams(
            collective_id=1, has_side_effects=True, vmem_limit_bytes=LAYER_VMEM
        ),
        name="layer_step",
    )(
        *(
            pltpu.with_memory_space_constraint(array, pltpu.HBM)
            for array in (
                parents, tokens, gate_bias, parents, gate_weight,
                norm_gain.reshape(heads, head_size), states,
                table.reshape(table.shape[0] // 8, 8, head_size), weights, out_weight,
            )
        ),
    ), cuts[-1][0]


def update_kernel(
    late, list_s, new_in, late_in, units, values, decays, layer_in, out_ref, layer_out, tail,
    out_sem, side_sem
):
    row_local, heads = new_in.shape[0], new_in.shape[1]
    device = lax.axis_index("rows")
    member, user = device % 4, device // 4
    layer_copy = pltpu.make_async_copy(layer_in, layer_out, side_sem.at[0])
    layer_copy.start()
    fronts = [
        pltpu.make_async_copy(
            new_in.at[row, pl.ds(0, late)], out_ref.at[row, pl.ds(0, late)],
            side_sem.at[1 + row],
        )
        for row in range(row_local)
    ]
    for copy in fronts:
        copy.start()
    blocks = [
        lax.div(list_s[0, user, member * row_local + row], row_local) for row in range(row_local)
    ]
    span = pl.ds(late, heads - late)
    for row in range(row_local):
        partner = jnp.bitwise_xor(blocks[row], member)
        rank = jnp.int32(0)
        for earlier in range(row):
            rank = rank + (blocks[earlier] == blocks[row]).astype(jnp.int32)
        rank = jnp.minimum(rank, CAP - 1)

        @pl.when(partner < 2)
        def _():
            pltpu.make_async_copy(
                new_in.at[row, span], out_ref.at[row, span], out_sem.at[row]
            ).start()

        @pl.when(partner > 1)
        def _():
            columns = jnp.transpose(units[row])
            value, decay = values[row], decays[row]
            for head in range(late, heads):
                fresh = columns[:, head : head + 1] * value[head : head + 1, :]
                prior = late_in[(partner - 2) * CAP + rank, head - late].astype(jnp.float32)
                tail[row, head - late] = (decay[head : head + 1, :] * prior + fresh).astype(
                    jnp.bfloat16
                )
            pltpu.make_async_copy(tail.at[row], out_ref.at[row, span], out_sem.at[row]).start()

    for row in range(row_local):
        pltpu.make_async_copy(tail.at[row], out_ref.at[row, span], out_sem.at[row]).wait()
    for copy in fronts:
        copy.wait()
    layer_copy.wait()


def update(late, parents, parts):
    states, layer_in = parts[0], parts[-1]
    row_local, heads = states.shape[:2]
    return pl.pallas_call(
        functools.partial(update_kernel, late),
        out_shape=(
            jax.ShapeDtypeStruct(states.shape, states.dtype),
            jax.ShapeDtypeStruct(layer_in.shape, layer_in.dtype),
        ),
        in_specs=[SM] + [VM] * len(parts),
        out_specs=(ANY, ANY),
        scratch_shapes=[
            pltpu.VMEM((row_local, heads - late) + states.shape[2:], states.dtype),
            pltpu.SemaphoreType.DMA((row_local,)),
            pltpu.SemaphoreType.DMA((row_local + 1,)),
        ],
        compiler_params=pltpu.CompilerParams(vmem_limit_bytes=UPDATE_VMEM),
        cost_estimate=pl.CostEstimate(
            flops=math.prod(states.shape),
            bytes_accessed=2 * math.prod(states.shape),
            transcendentals=0,
        ),
        name="update_states",
    )(parents, *(pltpu.with_memory_space_constraint(part, pltpu.VMEM) for part in parts))


def fast(
    token_ids, parents, states, embed_table, qkv_weight, gate_weight, gate_bias, norm_gain,
    out_weight
):
    count = lax.axis_size("rows")
    parts, late = layer(
        parents, token_ids, gate_bias, gate_weight, norm_gain, states, embed_table,
        jnp.transpose(qkv_weight, (1, 0, 2)), out_weight, count,
    )
    state_now, layer_out = update(late, parents, parts)
    return (layer_out[None], state_now)


def from_partner(block, axis, stride):
    count = lax.axis_size(axis)
    route = []
    for low in range(count):
        high = low | 1 << stride
        if high != low and high < count:
            route += [(low, high), (high, low)]
    return lax.ppermute(block, axis, route)


def outgoing(state_now, parent_list, member, row_local, partner):
    target = jnp.bitwise_xor(member, partner)
    children = lax.dynamic_slice_in_dim(parent_list, target * row_local, row_local, 0)
    needed = children // row_local == member
    rank_index = jnp.cumsum(needed.astype(jnp.int32)) - 1
    slot_ids = jnp.arange(CAP, dtype=jnp.int32)
    chosen = jnp.sum(
        jnp.where(
            needed[None, :] & (rank_index[None, :] == slot_ids[:, None]),
            (children % row_local)[None, :],
            0,
        ),
        axis=1,
    )
    return jnp.take(state_now, chosen, axis=0)


def route(state_now, parent_list, member, row_local):
    first_out = outgoing(state_now, parent_list, member, row_local, 1)
    second_out = outgoing(state_now, parent_list, member, row_local, 2)
    corner_out = outgoing(state_now, parent_list, member, row_local, 3)
    got_one = from_partner(first_out, "rows", 0)
    got_two = from_partner(second_out, "rows", 1)
    relayed = from_partner(corner_out, "rows", 0)
    got_three = from_partner(relayed, "rows", 1)
    own_list = lax.dynamic_slice_in_dim(parent_list, member * row_local, row_local, 0)
    source = own_list // row_local
    partner = jnp.bitwise_xor(source, member)
    slot_index = jnp.arange(row_local, dtype=jnp.int32)
    earlier = (source[:, None] == source[None, :]) & (slot_index[:, None] > slot_index[None, :])
    rank_index = jnp.sum(earlier.astype(jnp.int32), axis=1)
    position = jnp.where(
        partner == 0, own_list % row_local, row_local + (partner - 1) * CAP + rank_index
    )
    pooled = jnp.concatenate([state_now, got_one, got_two, got_three], 0)
    return jnp.take(pooled, position, axis=0)


def per_device(
    token_ids,
    parents,
    states,
    embed_table,
    qkv_weight,
    gate_weight,
    gate_bias,
    norm_gain,
    out_weight,
):
    row_local = states.shape[0]
    heads = states.shape[1]
    head_size = states.shape[2]
    count = lax.axis_size("rows")
    if (
        embed_table.shape[1] == head_size
        and head_size % 128 == 0
        and count == heads
        and parents.shape[0] == 1
        and parents.shape[2] == 4 * row_local
        and parents.shape[1] * 4 == count
        and row_local % 8 == 0
        and heads % 16 == 0
        and math.prod(embed_table.shape) * 2 <= 1 << 24
        and math.prod(states.shape) * 2 <= 1 << 23
    ):
        return fast(
            token_ids, parents, states, embed_table, qkv_weight, gate_weight, gate_bias,
            norm_gain, out_weight
        )
    width = heads * head_size
    column_local = embed_table.shape[1]
    row_total = token_ids.shape[1]
    device = lax.axis_index("rows")
    member = device % 4
    user_index = device // 4
    weight_flat = qkv_weight.reshape(qkv_weight.shape[0], 3 * column_local)
    local_columns = jnp.take(embed_table, token_ids, axis=0)
    every_proj = jnp.einsum(
        "...rc,cf->...rf",
        lax.all_gather(local_columns, "rows", axis=2, tiled=True),
        weight_flat,
        preferred_element_type=jnp.float32,
    )
    state_now = states
    step_proj = every_proj[0]
    projected = step_proj.astype(jnp.bfloat16).reshape(row_total, 3, column_local)
    mine = lax.all_to_all(projected, "rows", split_axis=0, concat_axis=2, tiled=True)
    queries = mine[:, 0].reshape(row_local, heads, head_size)
    key_float = mine[:, 1].reshape(row_local, heads, head_size).astype(jnp.float32)
    values = mine[:, 2].reshape(row_local, heads, head_size).astype(jnp.float32)
    gate_logit = jnp.sum(key_float * gate_weight, axis=-1) / math.sqrt(head_size) + gate_bias
    decay_rate = jax.nn.sigmoid(gate_logit)
    key_unit = key_float * lax.rsqrt(jnp.sum(key_float * key_float, axis=-1, keepdims=True) + 1e-06)
    parent_list = lax.dynamic_index_in_dim(parents[0], user_index, 0, keepdims=False)
    prior_state = route(state_now, parent_list, member, row_local)
    new_state = (
        decay_rate[:, :, None, None] * prior_state.astype(jnp.float32)
        + key_unit[:, :, :, None] * values[:, :, None, :]
    )
    state_now = new_state.astype(jnp.bfloat16)
    readout = jnp.einsum("rhd,rhde->rhe", queries, state_now, preferred_element_type=jnp.float32)
    scaled = readout * lax.rsqrt(jnp.mean(readout * readout, axis=-1, keepdims=True) + 1e-05)
    normed = (scaled.reshape(row_local, width) * norm_gain).astype(jnp.bfloat16)
    attention = jnp.dot(
        lax.all_gather(normed, "rows", axis=0, tiled=True),
        out_weight,
        preferred_element_type=jnp.float32,
    )
    outputs = [(local_columns[0].astype(jnp.float32) + attention).astype(jnp.bfloat16)]
    return (jnp.stack(outputs), state_now)


def solution(mesh):
    placed = (
        P(None, "groups"),
        P(None, "groups", None),
        P(("groups", "rows"), None, None, None),
        P(None, "rows"),
        P(None, None, "rows"),
        P(),
        P(),
        P(),
        P(None, "rows"),
    )
    return jax.shard_map(
        per_device,
        mesh=mesh,
        in_specs=placed,
        out_specs=(P(None, "groups", "rows"), P(("groups", "rows"), None, None, None)),
        check_vma=False,
    )
```
